32 devices in a mesh: ctx: 8 (over y, x, core), grp: 4 (over z).
Axes of the slice: x: 2, y: 2, z: 4, core: 2. Of those that a mesh axis runs over, the one named last changes fastest.
Arguments:
- query_in: bfloat16 [8192, 4096], P('ctx', 'grp'), may hold values from -6 to 6
- key_in: bfloat16 [8192, 4096], P('ctx', 'grp'), may hold values from -6 to 6
- value_in: bfloat16 [8192, 4096], P('ctx', 'grp'), may hold values from -6 to 6
- residues: float32 [256, 16], P('grp'), may hold values from -1.5 to 1.5
- decay_time: float32 [256, 16], P('grp'), may hold values from 20 to 32768
- skip_gain: float32 [4096], P('grp'), may hold values from 0.5 to 1.5
- out_proj: bfloat16 [4096, 4096], P('ctx', 'grp'), may hold values from -0.09375 to 0.09375
- doc_lengths: int32 [4], replicated, may hold values from 1 to 4096, 8192 in all
- grad_out: bfloat16 [8192, 4096], P('ctx', 'grp'), may hold values from -6 to 6
Outputs:
- mixed_out: bfloat16 [8192, 4096], P('ctx', 'grp')
- grad_query: bfloat16 [8192, 4096], P('ctx', 'grp')
- grad_key: bfloat16 [8192, 4096], P('ctx', 'grp')
- grad_value: bfloat16 [8192, 4096], P('ctx', 'grp')
- grad_proj: float32 [4096, 4096], P('ctx', 'grp')
The draws below stay inside these ranges and needn't reach their ends.
Inputs may be any that keep to these rules, and one draw needn't show every extreme that they name: `doc_lengths`: document lengths in window order, summing to 8192; the longest is exactly 4096.
All inputs are finite; a program needn't handle non-finite values.
Results may differ from the reference program's by a relative error of at most 0.013.
Values may be sent and summed in bfloat16 or wider, within the bound.
A program may use at most 192 MiB of HBM per device.

```python
import math
import jax
import jax.numpy as jnp
import numpy as np
from jax import lax

D = 4096
GROUP = 16
ORDER = 16
NDOCS = 4
GROUPS = 256
TOKENS = 8192
N_GRP = 4


def level_of(rng, dims, split, low, top_value):
    loudness = 1.0
    for position, parts in split:
        draws = jax.random.uniform(jax.random.fold_in(jax.random.fold_in(rng, 6), position), (parts,), jnp.float32, low / len(split), top_value / len(split))
        loudness = loudness * jnp.repeat(jnp.exp(draws), dims[position] // parts).reshape((-1,) + (1,) * (len(dims) - 1 - position))
    return loudness


def profile(count, total, limit, lean):
    portions = [(1 << 20) // math.isqrt(rank ** lean) + 1 for rank in range(2, count + 1)]
    rest, given = total - limit - (count - 1), [1] * (count - 1)
    while rest > 0:
        free = [i for i in range(count - 1) if given[i] < limit]
        mass, left = sum([portions[i] for i in free]), rest
        for i in free:
            more = min(limit - given[i], max(1, left * portions[i] // mass), rest)
            given[i] = given[i] + more
            rest = rest - more
    return np.array([limit] + given)


def uneven_parts(own_key, number_of, total, bound, skew):
    if number_of == 2:
        one = jax.random.randint(own_key, (), max(1, total - bound), min(bound, total - 1) + 1)
        return jnp.stack([one, total - one])
    lengths = jnp.asarray(profile(number_of, total, bound, skew), jnp.int32)
    couples = (number_of - 1) // 2
    giver, sink = lengths[1:1 + 2 * couples:2], lengths[2:2 + 2 * couples:2]
    margin = jnp.minimum(giver - 1, bound - sink)
    moved = jax.random.randint(jax.random.fold_in(own_key, 1), (couples,), 0, 1 << 20) % (margin + 1)
    lengths = lengths.at[1:1 + 2 * couples:2].set(giver - moved).at[2:2 + 2 * couples:2].set(sink + moved)
    return lengths[jax.random.permutation(jax.random.fold_in(own_key, 2), number_of)]


def gaussian(rng, shape, scale, bound, cuts=(), kind=jnp.bfloat16):
    factor_of = level_of(rng, shape, cuts, -0.22, 0.18) if cuts else 1.0
    values = jax.random.normal(rng, shape, jnp.float32) * scale * factor_of
    return jnp.minimum(jnp.maximum(values, -bound), bound).astype(kind)


def setup_inputs(seed: int = 0) -> dict:
    splits = jax.random.split(jax.random.key(seed), 10)
    query_in = gaussian(splits[0], (TOKENS, D), 1.0, 6.0, ((0, 8), (1, 4)))
    key_in = gaussian(splits[1], (TOKENS, D), 1.0, 6.0, ((0, 8), (1, 4)))
    value_in = gaussian(splits[2], (TOKENS, D), 1.0, 6.0, ((0, 8), (1, 4)))
    residues = gaussian(splits[3], (GROUPS, ORDER), ORDER ** -0.5, 1.5, ((0, 4),), jnp.float32)
    decay_time = jnp.clip(jnp.exp(math.log(32768.0) - 7.4014754 * jax.random.uniform(splits[4], (GROUPS, ORDER), jnp.float32) ** level_of(splits[4], (GROUPS, ORDER), ((0, 4),), -0.2, 0.2)), 20.0, 32768.0)
    skip_gain = jnp.clip(0.5 + 1.0 * jax.random.uniform(splits[5], (D,), jnp.float32) ** level_of(splits[5], (D,), ((0, 4),), -0.2, 0.2), 0.5, 1.5)
    out_proj = gaussian(splits[6], (D, D), D ** -0.5, 0.09375, ((0, 8), (1, 4)))
    doc_lengths = uneven_parts(splits[7], NDOCS, TOKENS, TOKENS // 2, 2).astype(jnp.int32)
    grad_out = gaussian(splits[8], (TOKENS, D), 1.0, 6.0, ((0, 8), (1, 4)))
    return {"query_in": query_in, "key_in": key_in, "value_in": value_in, "residues": residues, "decay_time": decay_time, "skip_gain": skip_gain, "out_proj": out_proj, "doc_lengths": doc_lengths, "grad_out": grad_out}


def doc_index(doc_lengths, amount):
    starts = jnp.cumsum(doc_lengths) - doc_lengths
    where_now = jnp.arange(amount, dtype=jnp.int32)
    return lax.optimization_barrier(jnp.sum((starts[None, :] <= where_now[:, None]).astype(jnp.int32), axis=1)) - 1

def reference(query_in, key_in, value_in, residues, decay_time, skip_gain, out_proj, doc_lengths, grad_out):
    decay_factor = jnp.exp(-1.0 / decay_time)
    residue_scaled = residues * jnp.sqrt(-jnp.expm1(-2.0 / decay_time))
    factor_chan = jnp.repeat(decay_factor, GROUP, axis=0)
    scaled_chan = jnp.repeat(residue_scaled, GROUP, axis=0)
    doc_ids = doc_index(doc_lengths, TOKENS)
    prior_ids = jnp.concatenate([jnp.array([-1], jnp.int32), doc_ids[:-1]])
    resets = doc_ids != prior_ids
    query_f = query_in.astype(jnp.float32)
    key_f = key_in.astype(jnp.float32)
    value_f = value_in.astype(jnp.float32)
    product = (key_f * value_f).astype(jnp.bfloat16)
    product_f = product.astype(jnp.float32)

    def forward_step(state, item):
        line, fresh = item
        state = jnp.where(fresh, 0.0, factor_chan * state) + line[:, None]
        return (state, lax.optimization_barrier(jnp.sum(scaled_chan * state, axis=1)))
    _, convolved = lax.scan(forward_step, jnp.zeros((D, ORDER), jnp.float32), (product_f, resets))
    filtered = convolved + skip_gain * product_f
    gated = (query_f * filtered).astype(jnp.bfloat16)
    width = D // N_GRP
    running = jnp.zeros((TOKENS, D), jnp.float32)
    for number in range(N_GRP):
        partial_value = jnp.dot(gated[:, number * width:(number + 1) * width], out_proj[:, number * width:(number + 1) * width].T, preferred_element_type=jnp.float32)
        running = running + lax.optimization_barrier(partial_value.astype(jnp.bfloat16)).astype(jnp.float32)
    mixed_out = running.astype(jnp.bfloat16)
    grad_gated = jnp.dot(grad_out, out_proj, preferred_element_type=jnp.float32)
    grad_query = (grad_gated * filtered).astype(jnp.bfloat16)
    grad_filtered = grad_gated * query_f
    resets_next = jnp.concatenate([resets[1:], jnp.array([True])])

    def backward_step(carry, item):
        line, cut = item
        carry = scaled_chan * line[:, None] + jnp.where(cut, 0.0, factor_chan * carry)
        return (carry, lax.optimization_barrier(jnp.sum(carry, axis=1)))
    _, returned = lax.scan(backward_step, jnp.zeros((D, ORDER), jnp.float32), (grad_filtered, resets_next), reverse=True)
    grad_product = returned + skip_gain * grad_filtered
    grad_key = (grad_product * value_f).astype(jnp.bfloat16)
    grad_value = (grad_product * key_f).astype(jnp.bfloat16)
    grad_proj = jnp.dot(grad_out.T, gated, preferred_element_type=jnp.float32)
    return (mixed_out, grad_query, grad_key, grad_value, grad_proj)
```

```python
import functools

import jax
import jax.numpy as jnp
from jax import lax
from jax.experimental import pallas as pl
from jax.experimental.pallas import tpu as pltpu
from jax.sharding import PartitionSpec as P

LANES = 128
BLOCK = 128
F32 = jnp.float32
BF16 = jnp.bfloat16


def doc_index(starts, where_now):
    return jnp.sum((starts[None, :] <= where_now[:, None]).astype(jnp.int32), axis=1) - 1


def pick(stacked, count, rows, members):
    lane_filter = lax.broadcasted_iota(jnp.int32, (rows, LANES), 1) // members
    out = stacked[:rows]
    for g in range(1, count):
        out = jnp.where(lane_filter == g, stacked[g * rows:(g + 1) * rows], out)
    return out


def summary_kernel(count, poles, members, a_ref, b_ref, leave_ref, out_ref):
    line = (a_ref[...].astype(F32) * b_ref[...].astype(F32)).astype(BF16)
    stacked = jnp.dot(leave_ref[...], line, preferred_element_type=F32)
    out_ref[...] = pick(stacked, count, poles, members).astype(out_ref.dtype)


def summarize(a, b, leave, poles, members):
    rows, channels = a.shape
    count = LANES // members
    return pl.pallas_call(
        functools.partial(summary_kernel, count, poles, members),
        grid=(channels // LANES,),
        in_specs=[
            pl.BlockSpec((rows, LANES), lambda j: (0, j)),
            pl.BlockSpec((rows, LANES), lambda j: (0, j)),
            pl.BlockSpec((count * poles, rows), lambda j: (j, 0)),
        ],
        out_specs=pl.BlockSpec((poles, LANES), lambda j: (0, j)),
        out_shape=jax.ShapeDtypeStruct((poles, channels), BF16),
        cost_estimate=pl.CostEstimate(
            flops=2 * rows * channels * poles * count,
            bytes_accessed=rows * channels * 8,
            transcendentals=0,
        ),
    )(a, b, leave)


def convolve(reverse, count, poles, members, blocks, line_of, emit, lag_ref, gain_ref, mask_ref,
             leave_ref, alive_ref, across_ref, alive_across_ref, enter_ref, base):
    for g in range(count):
        row = jnp.broadcast_to(lag_ref[g:g + 1, :], (BLOCK, LANES))
        matrix = pltpu.roll(row, 0, 1, stride=1, stride_axis=0)
        base[g * BLOCK:(g + 1) * BLOCK, :LANES] = matrix.astype(BF16)
    base[:, LANES:] = gain_ref[...]
    state = enter_ref[...]
    for step in range(blocks):
        b = blocks - 1 - step if reverse else step
        line = line_of(b)
        low = line.astype(BF16)
        mask = mask_ref[b]
        left = (base[...].reshape(count, BLOCK, LANES + poles) * mask[None]).reshape(
            count * BLOCK, LANES + poles
        )
        right = jnp.concatenate([low, state.astype(BF16)], axis=0)
        result = pick(
            jnp.dot(left, right, preferred_element_type=F32), count, BLOCK, members
        )
        emit(b, line, result)
        if step < blocks - 1:
            gone = leave_ref[...] * alive_ref[b:b + 1, :]
            fresh = pick(
                jnp.dot(gone.astype(BF16), low, preferred_element_type=F32), count, poles, members
            )
            state = across_ref[...] * alive_across_ref[b:b + 1, :] * state + fresh


def forward_kernel(count, poles, members, blocks, query, key, value, skip, lag, gain, mask, leave,
                   alive, across, alive_across, enter, filtered, gated, base):
    def rows(b):
        return pl.ds(b * BLOCK, BLOCK)

    def line_of(b):
        return (key[rows(b), :].astype(F32) * value[rows(b), :].astype(F32)).astype(BF16).astype(F32)

    def emit(b, line, result):
        result = result + skip[...] * line
        filtered[rows(b), :] = result
        gated[rows(b), :] = (query[rows(b), :].astype(F32) * result).astype(BF16)

    convolve(False, count, poles, members, blocks, line_of, emit, lag, gain, mask, leave, alive,
             across, alive_across, enter, base)


def backward_kernel(count, poles, members, blocks, query, key, value, grad_gated, filtered, skip,
                    lag, gain, mask, leave, alive, across, alive_across, enter, grad_query,
                    grad_key, grad_value, base):
    def rows(b):
        return pl.ds(b * BLOCK, BLOCK)

    def line_of(b):
        grad = grad_gated[rows(b), :]
        grad_query[rows(b), :] = (grad * filtered[rows(b), :]).astype(BF16)
        return grad * query[rows(b), :].astype(F32)

    def emit(b, line, result):
        result = result + skip[...] * line
        grad_key[rows(b), :] = (result * value[rows(b), :].astype(F32)).astype(BF16)
        grad_value[rows(b), :] = (result * key[rows(b), :].astype(F32)).astype(BF16)

    convolve(True, count, poles, members, blocks, line_of, emit, lag, gain, mask, leave, alive,
             across, alive_across, enter, base)


def run_conv(kernel, wide, skip, tables, enter, out_types, poles, members):
    rows, channels = wide[0].shape
    count = LANES // members
    blocks = rows // BLOCK
    column = pl.BlockSpec((rows, LANES), lambda j: (0, j))
    lag, gain, mask, leave, alive, across, alive_across = tables
    return pl.pallas_call(
        functools.partial(kernel, count, poles, members, blocks),
        grid=(channels // LANES,),
        in_specs=[column] * len(wide) + [
            pl.BlockSpec((1, LANES), lambda j: (0, j)),
            pl.BlockSpec((count, BLOCK), lambda j: (j, 0)),
            pl.BlockSpec((count * BLOCK, poles), lambda j: (j, 0)),
            pl.BlockSpec((blocks, BLOCK, BLOCK + poles), lambda j: (0, 0, 0)),
            pl.BlockSpec((count * poles, BLOCK), lambda j: (j, 0)),
            pl.BlockSpec((blocks, BLOCK), lambda j: (0, 0)),
            pl.BlockSpec((poles, LANES), lambda j: (0, j)),
            pl.BlockSpec((blocks, LANES), lambda j: (0, 0)),
            pl.BlockSpec((poles, LANES), lambda j: (0, j)),
        ],
        out_specs=[column] * len(out_types),
        out_shape=[jax.ShapeDtypeStruct((rows, channels), kind) for kind in out_types],
        scratch_shapes=[pltpu.VMEM((count * BLOCK, BLOCK + poles), BF16)],
        cost_estimate=pl.CostEstimate(
            flops=16 * rows * channels * BLOCK * 2, bytes_accessed=rows * channels * 14, transcendentals=0
        ),
    )(*wide, skip, lag, gain, mask, leave, alive, across, alive_across, enter)


def swap(value, flip, size):
    return lax.ppermute(value, "ctx", [(i, i ^ flip) for i in range(size)])


def gather_rows(own, size, me):
    if size != 8:
        return lax.all_gather(own, "ctx", axis=0, tiled=True)
    half = own.shape[0] // 2
    by_x, by_y = swap(own, 2, size), swap(own, 4, size)
    first, second = swap(by_x[:half], 4, size), swap(by_y[half:], 2, size)
    parts = {0: [own], 2: [by_x], 4: [by_y], 6: [first, second]}
    for flip in (0, 2, 4, 6):
        parts[flip ^ 1] = [swap(part, 1, size) for part in parts[flip]]
    rows, columns = own.shape
    whole = jnp.zeros((rows * size, columns), own.dtype)
    for flip, pieces in parts.items():
        at = (me ^ flip) * rows
        for piece in pieces:
            whole = lax.dynamic_update_slice(whole, piece, (at, 0))
            at = at + piece.shape[0]
    return whole


def scatter_terms(grad_full, gated, size, me):
    contract = (((0,), (0,)), ((), ()))
    if size != 8:
        term = lax.dot_general(grad_full, gated, contract, preferred_element_type=F32).astype(BF16)
        return term, lambda term: lax.psum_scatter(term, "ctx", scatter_dimension=0, tiled=True).astype(F32)
    width = grad_full.shape[1] // size

    def chunk(flip):
        part = lax.dynamic_slice_in_dim(grad_full, (me ^ flip) * width, width, axis=1)
        return lax.dot_general(part, gated, contract, preferred_element_type=F32).astype(BF16)

    terms = {flip: chunk(flip) for flip in (7, 3, 5, 1, 6, 2, 4, 0)}

    def finish(terms):
        half = gated.shape[1] // 2
        sums = {}
        for flip in (6, 2, 4, 0):
            sums[flip] = terms[flip].astype(F32) + swap(terms[flip ^ 1], 1, size).astype(F32)

        def route(columns, near, far):
            far_sum = sums[far][:, columns] + swap(sums[6][:, columns].astype(BF16), near, size).astype(F32)
            own_sum = sums[0][:, columns] + swap(sums[near][:, columns].astype(BF16), near, size).astype(F32)
            return own_sum + swap(far_sum.astype(BF16), far, size).astype(F32)

        return jnp.concatenate([route(slice(0, half), 2, 4), route(slice(half, None), 4, 2)], axis=1)

    return terms, finish


def local(
    query_in, key_in, value_in, residues, decay_time, skip_gain, out_proj, doc_lengths, grad_out
):
    rows, channels = query_in.shape
    filters, poles = residues.shape
    members = channels // filters
    blocks = rows // BLOCK
    size, me = lax.axis_size("ctx"), lax.axis_index("ctx")
    gathered = gather_rows(out_proj, size, me)
    grad_full = lax.all_gather(grad_out, "grp", axis=1, tiled=True)

    starts = jnp.cumsum(doc_lengths) - doc_lengths
    flat_ids = doc_index(starts, me * rows + jnp.arange(rows, dtype=jnp.int32))
    ids = flat_ids.reshape(blocks, BLOCK)
    firsts, lasts = ids[:, 0], ids[:, -1]
    before = doc_index(starts, me * rows - 1 + BLOCK * jnp.arange(blocks + 1, dtype=jnp.int32))
    after = doc_index(starts, me * rows + BLOCK * jnp.arange(1, blocks + 1, dtype=jnp.int32))
    ends = doc_index(starts, rows * jnp.arange(1, size + 1, dtype=jnp.int32) - 1)
    opens = doc_index(starts, rows * jnp.arange(size, dtype=jnp.int32))
    rate = 1.0 / decay_time
    beta = residues * jnp.sqrt(-jnp.expm1(-2.0 * rate))
    lags = jnp.arange(BLOCK, dtype=F32)
    rate_chan = jnp.repeat(rate.T, members, axis=1)
    response = jnp.sum(beta[:, :, None] * jnp.exp(-lags[None, None, :] * rate[:, :, None]), axis=1)
    mirrored = jnp.concatenate([response[:, :1], response[:, :0:-1]], axis=1)
    gain = beta[:, None, :] * jnp.exp(-(lags + 1.0)[None, :, None] * rate[:, None, :])
    gain_rev = gain[:, ::-1, :]
    leave_rev = jnp.exp(-lags[None, :] * rate.reshape(-1, 1))
    leave = jnp.exp(-(BLOCK - 1.0 - lags)[None, :] * rate.reshape(-1, 1))
    across = jnp.exp(-BLOCK * rate_chan)
    same = ids[:, :, None] == ids[:, None, :]
    place = jnp.arange(BLOCK)
    causal = place[:, None] >= place[None, :]

    def mask_of(order, alive):
        tail = jnp.broadcast_to(alive[:, :, None], (blocks, BLOCK, poles))
        return jnp.concatenate([same & order[None], tail], axis=2).astype(BF16)

    def spread(flags):
        return jnp.broadcast_to(flags.astype(F32)[:, None], (blocks, LANES))

    forward = (
        mirrored,
        gain.reshape(-1, poles).astype(BF16),
        mask_of(causal, ids == before[:blocks, None]),
        leave,
        (ids == lasts[:, None]).astype(F32),
        across,
        spread(before[:blocks] == lasts),
    )
    backward = (
        response,
        gain_rev.reshape(-1, poles).astype(BF16),
        mask_of(causal.T, ids == after[:, None]),
        leave_rev,
        (ids == firsts[:, None]).astype(F32),
        across,
        spread(after == firsts),
    )
    steps = jnp.arange(rows, dtype=F32)
    whole_leave = jnp.exp(-(rows - 1.0 - steps)[None, :] * rate.reshape(-1, 1))
    whole_leave = (whole_leave * (flat_ids == flat_ids[-1])[None, :]).astype(BF16)
    whole_leave_rev = jnp.exp(-steps[None, :] * rate.reshape(-1, 1))
    whole_leave_rev = (whole_leave_rev * (flat_ids == flat_ids[0])[None, :]).astype(BF16)

    def incoming(state, distance, alive):
        everything = lax.all_gather(state, "ctx").astype(F32)
        gap = jnp.maximum(distance, 0).astype(F32) * rows
        weight = jnp.exp(-gap[:, None, None] * rate_chan[None])
        kept = (alive & (distance >= 0))[:, None, None]
        return jnp.sum(jnp.where(kept, weight * everything, 0.0), axis=0)

    devices = jnp.arange(size, dtype=jnp.int32)
    skip = skip_gain[None, :]
    state = summarize(key_in, value_in, whole_leave, poles, members)
    enter = incoming(state, me - 1 - devices, ends == before[0])
    filtered, gated = run_conv(
        forward_kernel, (query_in, key_in, value_in), skip, forward, enter, (F32, BF16), poles, members
    )
    partial_value = lax.dot_general(
        gated, gathered, (((1,), (1,)), ((), ())), preferred_element_type=F32
    ).astype(BF16)
    mixed_out = lax.psum_scatter(partial_value, "grp", scatter_dimension=1, tiled=True)
    terms, finish = scatter_terms(grad_full, gated, size, me)
    terms, grad_full, gathered = lax.optimization_barrier((terms, grad_full, gathered))
    grad_proj = finish(terms)
    grad_gated = jnp.dot(grad_full, gathered, preferred_element_type=F32)
    state = summarize(grad_gated, query_in, whole_leave_rev, poles, members)
    leaving = incoming(state, devices - 1 - me, opens == after[-1])
    grad_query, grad_key, grad_value = run_conv(
        backward_kernel, (query_in, key_in, value_in, grad_gated, filtered), skip, backward,
        leaving, (BF16, BF16, BF16), poles, members
    )
    return (mixed_out, grad_query, grad_key, grad_value, grad_proj)


def solution(mesh):
    return jax.shard_map(
        local,
        mesh=mesh,
        in_specs=(
            P("ctx", "grp"),
            P("ctx", "grp"),
            P("ctx", "grp"),
            P("grp", None),
            P("grp", None),
            P("grp"),
            P("ctx", "grp"),
            P(),
            P("ctx", "grp"),
        ),
        out_specs=(
            P("ctx", "grp"),
            P("ctx", "grp"),
            P("ctx", "grp"),
            P("ctx", "grp"),
            P("ctx", "grp"),
        ),
        check_vma=False,
    )
```

```python
import functools

import jax
import jax.numpy as jnp
from jax import lax
from jax.experimental import pallas as pl
from jax.experimental.pallas import tpu as pltpu
from jax.sharding import PartitionSpec as P

LANES = 128
BLOCK = 128
F32 = jnp.float32
BF16 = jnp.bfloat16


def doc_index(starts, where_now):
    return jnp.sum((starts[None, :] <= where_now[:, None]).astype(jnp.int32), axis=1) - 1


def pick(stacked, count, rows, members):
    lane_filter = lax.broadcasted_iota(jnp.int32, (rows, LANES), 1) // members
    out = stacked[:rows]
    for g in range(1, count):
        out = jnp.where(lane_filter == g, stacked[g * rows:(g + 1) * rows], out)
    return out


def summary_kernel(count, poles, members, a_ref, b_ref, leave_ref, out_ref):
    line = (a_ref[...].astype(F32) * b_ref[...].astype(F32)).astype(BF16)
    stacked = jnp.dot(leave_ref[...], line, preferred_element_type=F32)
    out_ref[...] = pick(stacked, count, poles, members).astype(out_ref.dtype)


def summarize(a, b, leave, poles, members):
    rows, channels = a.shape
    count = LANES // members
    return pl.pallas_call(
        functools.partial(summary_kernel, count, poles, members),
        grid=(channels // LANES,),
        in_specs=[
            pl.BlockSpec((rows, LANES), lambda j: (0, j)),
            pl.BlockSpec((rows, LANES), lambda j: (0, j)),
            pl.BlockSpec((count * poles, rows), lambda j: (j, 0)),
        ],
        out_specs=pl.BlockSpec((poles, LANES), lambda j: (0, j)),
        out_shape=jax.ShapeDtypeStruct((poles, channels), BF16),
        cost_estimate=pl.CostEstimate(
            flops=2 * rows * channels * poles * count,
            bytes_accessed=rows * channels * 8,
            transcendentals=0,
        ),
    )(a, b, leave)


def convolve(reverse, count, poles, members, blocks, line_of, emit, lag_ref, gain_ref, mask_ref,
             leave_ref, alive_ref, across_ref, alive_across_ref, enter_ref, base):
    for g in range(count):
        row = jnp.broadcast_to(lag_ref[g:g + 1, :], (BLOCK, LANES))
        matrix = pltpu.roll(row, 0, 1, stride=1, stride_axis=0)
        base[g * BLOCK:(g + 1) * BLOCK, :LANES] = matrix.astype(BF16)
    base[:, LANES:] = gain_ref[...]
    state = enter_ref[...]
    for step in range(blocks):
        b = blocks - 1 - step if reverse else step
        line = line_of(b)
        low = line.astype(BF16)
        mask = mask_ref[b]
        left = (base[...].reshape(count, BLOCK, LANES + poles) * mask[None]).reshape(
            count * BLOCK, LANES + poles
        )
        right = jnp.concatenate([low, state.astype(BF16)], axis=0)
        result = pick(
            jnp.dot(left, right, preferred_element_type=F32), count, BLOCK, members
        )
        emit(b, line, result)
        if step < blocks - 1:
            gone = leave_ref[...] * alive_ref[b:b + 1, :]
            fresh = pick(
                jnp.dot(gone.astype(BF16), low, preferred_element_type=F32), count, poles, members
            )
            state = across_ref[...] * alive_across_ref[b:b + 1, :] * state + fresh


def forward_kernel(count, poles, members, blocks, query, key, value, skip, lag, gain, mask, leave,
                   alive, across, alive_across, enter, filtered, gated, base):
    def rows(b):
        return pl.ds(b * BLOCK, BLOCK)

    def line_of(b):
        return (key[rows(b), :].astype(F32) * value[rows(b), :].astype(F32)).astype(BF16).astype(F32)

    def emit(b, line, result):
        result = result + skip[...] * line
        filtered[rows(b), :] = result
        gated[rows(b), :] = (query[rows(b), :].astype(F32) * result).astype(BF16)

    convolve(False, count, poles, members, blocks, line_of, emit, lag, gain, mask, leave, alive,
             across, alive_across, enter, base)


def backward_kernel(count, poles, members, blocks, query, key, value, grad_gated, filtered, skip,
                    lag, gain, mask, leave, alive, across, alive_across, enter, grad_query,
                    grad_key, grad_value, base):
    def rows(b):
        return pl.ds(b * BLOCK, BLOCK)

    def line_of(b):
        grad = grad_gated[rows(b), :]
        grad_query[rows(b), :] = (grad * filtered[rows(b), :]).astype(BF16)
        return grad * query[rows(b), :].astype(F32)

    def emit(b, line, result):
        result = result + skip[...] * line
        grad_key[rows(b), :] = (result * value[rows(b), :].astype(F32)).astype(BF16)
        grad_value[rows(b), :] = (result * key[rows(b), :].astype(F32)).astype(BF16)

    convolve(True, count, poles, members, blocks, line_of, emit, lag, gain, mask, leave, alive,
             across, alive_across, enter, base)


def run_conv(kernel, wide, skip, tables, enter, out_types, poles, members):
    rows, channels = wide[0].shape
    count = LANES // members
    blocks = rows // BLOCK
    column = pl.BlockSpec((rows, LANES), lambda j: (0, j))
    lag, gain, mask, leave, alive, across, alive_across = tables
    return pl.pallas_call(
        functools.partial(kernel, count, poles, members, blocks),
        grid=(channels // LANES,),
        in_specs=[column] * len(wide) + [
            pl.BlockSpec((1, LANES), lambda j: (0, j)),
            pl.BlockSpec((count, BLOCK), lambda j: (j, 0)),
            pl.BlockSpec((count * BLOCK, poles), lambda j: (j, 0)),
            pl.BlockSpec((blocks, BLOCK, BLOCK + poles), lambda j: (0, 0, 0)),
            pl.BlockSpec((count * poles, BLOCK), lambda j: (j, 0)),
            pl.BlockSpec((blocks, BLOCK), lambda j: (0, 0)),
            pl.BlockSpec((poles, LANES), lambda j: (0, j)),
            pl.BlockSpec((blocks, LANES), lambda j: (0, 0)),
            pl.BlockSpec((poles, LANES), lambda j: (0, j)),
        ],
        out_specs=[column] * len(out_types),
        out_shape=[jax.ShapeDtypeStruct((rows, channels), kind) for kind in out_types],
        scratch_shapes=[pltpu.VMEM((count * BLOCK, BLOCK + poles), BF16)],
        cost_estimate=pl.CostEstimate(
            flops=16 * rows * channels * BLOCK * 2, bytes_accessed=rows * channels * 14, transcendentals=0
        ),
    )(*wide, skip, lag, gain, mask, leave, alive, across, alive_across, enter)


def swap(value, flip, size):
    return lax.ppermute(value, "ctx", [(i, i ^ flip) for i in range(size)])


def gather_rows(own, size, me):
    if size != 8:
        return lax.all_gather(own, "ctx", axis=0, tiled=True)
    half = own.shape[0] // 2
    by_x, by_y = swap(own, 2, size), swap(own, 4, size)
    first, second = swap(by_x[:half], 4, size), swap(by_y[half:], 2, size)
    parts = {0: [own], 2: [by_x], 4: [by_y], 6: [first, second]}
    for flip in (0, 2, 4, 6):
        parts[flip ^ 1] = [swap(part, 1, size) for part in parts[flip]]
    rows, columns = own.shape
    whole = jnp.zeros((rows * size, columns), own.dtype)
    for flip, pieces in parts.items():
        at = (me ^ flip) * rows
        for piece in pieces:
            whole = lax.dynamic_update_slice(whole, piece, (at, 0))
            at = at + piece.shape[0]
    return whole


def after(value, *others):
    return lax.optimization_barrier((value, others))[0]


def scatter_columns(value, axis, before_last):
    size, me = lax.axis_size(axis), lax.axis_index(axis)
    width = value.shape[1] // size

    def own(position):
        start = jnp.clip(position, 0, size - 1) * width
        return lax.dynamic_slice_in_dim(value, start, width, axis=1).astype(F32)

    right = left = None
    for step in range(1, size):
        up, down = own(me + size - step), own(me - size + step)
        if step == size - 1:
            right, left = after((right, left), before_last)
        if right is not None:
            up, down = up + right.astype(F32), down + left.astype(F32)
        right = lax.ppermute(up.astype(BF16), axis, [(z, z + 1) for z in range(step)])
        left = lax.ppermute(
            down.astype(BF16), axis, [(size - 1 - z, size - 2 - z) for z in range(step)]
        )

    def finish(*others):
        last_right, last_left = after((right, left), others)
        return (own(me) + last_right.astype(F32) + last_left.astype(F32)).astype(BF16)

    return finish


def scatter_terms(grad_full, gated, size, me):
    contract = (((0,), (0,)), ((), ()))
    if size != 8:
        term = lax.dot_general(grad_full, gated, contract, preferred_element_type=F32).astype(BF16)
        return term, lambda term: lax.psum_scatter(term, "ctx", scatter_dimension=0, tiled=True).astype(F32)
    width = grad_full.shape[1] // size

    def chunk(flip):
        part = lax.dynamic_slice_in_dim(grad_full, (me ^ flip) * width, width, axis=1)
        return lax.dot_general(part, gated, contract, preferred_element_type=F32).astype(BF16)

    arriving = {flip: swap(chunk(flip ^ 1), 1, size) for flip in (6, 2, 4, 0)}
    terms = {flip: chunk(flip) for flip in (6, 2, 4, 0)}

    def finish(terms):
        half = gated.shape[1] // 2
        sums = {}
        for flip in (6, 2, 4, 0):
            sums[flip] = terms[flip].astype(F32) + arriving[flip].astype(F32)

        def route(columns, near, far):
            far_sum = sums[far][:, columns] + swap(sums[6][:, columns].astype(BF16), near, size).astype(F32)
            own_sum = sums[0][:, columns] + swap(sums[near][:, columns].astype(BF16), near, size).astype(F32)
            return own_sum + swap(far_sum.astype(BF16), far, size).astype(F32)

        return jnp.concatenate([route(slice(0, half), 2, 4), route(slice(half, None), 4, 2)], axis=1)

    return terms, finish


def local(
    query_in, key_in, value_in, residues, decay_time, skip_gain, out_proj, doc_lengths, grad_out
):
    rows, channels = query_in.shape
    filters, poles = residues.shape
    members = channels // filters
    blocks = rows // BLOCK
    size, me = lax.axis_size("ctx"), lax.axis_index("ctx")
    gathered = gather_rows(out_proj, size, me)
    grad_full = lax.all_gather(grad_out, "grp", axis=1, tiled=True)

    starts = jnp.cumsum(doc_lengths) - doc_lengths
    flat_ids = doc_index(starts, me * rows + jnp.arange(rows, dtype=jnp.int32))
    ids = flat_ids.reshape(blocks, BLOCK)
    firsts, lasts = ids[:, 0], ids[:, -1]
    before = doc_index(starts, me * rows - 1 + BLOCK * jnp.arange(blocks + 1, dtype=jnp.int32))
    following = doc_index(starts, me * rows + BLOCK * jnp.arange(1, blocks + 1, dtype=jnp.int32))
    ends = doc_index(starts, rows * jnp.arange(1, size + 1, dtype=jnp.int32) - 1)
    opens = doc_index(starts, rows * jnp.arange(size, dtype=jnp.int32))
    rate = 1.0 / decay_time
    beta = residues * jnp.sqrt(-jnp.expm1(-2.0 * rate))
    lags = jnp.arange(BLOCK, dtype=F32)
    rate_chan = jnp.repeat(rate.T, members, axis=1)
    response = jnp.sum(beta[:, :, None] * jnp.exp(-lags[None, None, :] * rate[:, :, None]), axis=1)
    mirrored = jnp.concatenate([response[:, :1], response[:, :0:-1]], axis=1)
    gain = beta[:, None, :] * jnp.exp(-(lags + 1.0)[None, :, None] * rate[:, None, :])
    gain_rev = beta[:, None, :] * jnp.exp(-(BLOCK - lags)[None, :, None] * rate[:, None, :])
    leave_rev = jnp.exp(-lags[None, :] * rate.reshape(-1, 1))
    leave = jnp.exp(-(BLOCK - 1.0 - lags)[None, :] * rate.reshape(-1, 1))
    across = jnp.exp(-BLOCK * rate_chan)
    same = ids[:, :, None] == ids[:, None, :]
    place = jnp.arange(BLOCK)
    causal = place[:, None] >= place[None, :]

    def mask_of(order, alive):
        tail = jnp.broadcast_to(alive[:, :, None], (blocks, BLOCK, poles))
        return jnp.concatenate([same & order[None], tail], axis=2).astype(BF16)

    def spread(flags):
        return jnp.broadcast_to(flags.astype(F32)[:, None], (blocks, LANES))

    forward = (
        mirrored,
        gain.reshape(-1, poles).astype(BF16),
        mask_of(causal, ids == before[:blocks, None]),
        leave,
        (ids == lasts[:, None]).astype(F32),
        across,
        spread(before[:blocks] == lasts),
    )
    backward = (
        response,
        gain_rev.reshape(-1, poles).astype(BF16),
        mask_of(causal.T, ids == following[:, None]),
        leave_rev,
        (ids == firsts[:, None]).astype(F32),
        across,
        spread(following == firsts),
    )
    steps = jnp.arange(rows, dtype=F32)
    whole_leave = jnp.exp(-(rows - 1.0 - steps)[None, :] * rate.reshape(-1, 1))
    whole_leave = (whole_leave * (flat_ids == flat_ids[-1])[None, :]).astype(BF16)
    whole_leave_rev = jnp.exp(-steps[None, :] * rate.reshape(-1, 1))
    whole_leave_rev = (whole_leave_rev * (flat_ids == flat_ids[0])[None, :]).astype(BF16)

    def incoming(state, distance, alive):
        everything = lax.all_gather(state, "ctx").astype(F32)
        gap = jnp.maximum(distance, 0).astype(F32) * rows
        weight = jnp.exp(-gap[:, None, None] * rate_chan[None])
        kept = (alive & (distance >= 0))[:, None, None]
        return jnp.sum(jnp.where(kept, weight * everything, 0.0), axis=0)

    devices = jnp.arange(size, dtype=jnp.int32)
    skip = skip_gain[None, :]
    state = summarize(key_in, value_in, whole_leave, poles, members)
    enter = incoming(state, me - 1 - devices, ends == before[0])
    filtered, gated = run_conv(
        forward_kernel, (query_in, key_in, value_in), skip, forward, enter, (F32, BF16), poles, members
    )
    partial_value = lax.dot_general(
        gated, gathered, (((1,), (1,)), ((), ())), preferred_element_type=F32
    ).astype(BF16)
    terms, finish = scatter_terms(grad_full, gated, size, me)
    finish_mixed = scatter_columns(partial_value, "grp", terms)
    terms, grad_full, gathered = lax.optimization_barrier((terms, grad_full, gathered))
    grad_proj = finish(terms)
    grad_gated = jnp.dot(grad_full, gathered, preferred_element_type=F32)
    state = summarize(grad_gated, query_in, whole_leave_rev, poles, members)
    leaving = incoming(state, devices - 1 - me, opens == following[-1])
    grad_query, grad_key, grad_value = run_conv(
        backward_kernel, (query_in, key_in, value_in, grad_gated, filtered), skip, backward,
        leaving, (BF16, BF16, BF16), poles, members
    )
    mixed_out = finish_mixed(grad_query)
    return (mixed_out, grad_query, grad_key, grad_value, grad_proj)


def solution(mesh):
    return jax.shard_map(
        local,
        mesh=mesh,
        in_specs=(
            P("ctx", "grp"),
            P("ctx", "grp"),
            P("ctx", "grp"),
            P("grp", None),
            P("grp", None),
            P("grp"),
            P("ctx", "grp"),
            P(),
            P("ctx", "grp"),
        ),
        out_specs=(
            P("ctx", "grp"),
            P("ctx", "grp"),
            P("ctx", "grp"),
            P("ctx", "grp"),
            P("ctx", "grp"),
        ),
        check_vma=False,
    )
```

```python
import functools

import jax
import jax.numpy as jnp
from jax import lax
from jax.experimental import pallas as pl
from jax.experimental.pallas import tpu as pltpu
from jax.sharding import PartitionSpec as P

LANES = 128
BLOCK = 128
F32 = jnp.float32
BF16 = jnp.bfloat16


def doc_index(starts, where_now):
    return jnp.sum((starts[None, :] <= where_now[:, None]).astype(jnp.int32), axis=1) - 1


def pick(stacked, count, rows, members):
    lane_filter = lax.broadcasted_iota(jnp.int32, (rows, LANES), 1) // members
    out = stacked[:rows]
    for g in range(1, count):
        out = jnp.where(lane_filter == g, stacked[g * rows:(g + 1) * rows], out)
    return out


def summary_kernel(count, poles, members, a_ref, b_ref, leave_ref, out_ref):
    line = (a_ref[...].astype(F32) * b_ref[...].astype(F32)).astype(BF16)
    stacked = jnp.dot(leave_ref[...], line, preferred_element_type=F32)
    out_ref[...] = pick(stacked, count, poles, members).astype(out_ref.dtype)


def summarize(a, b, leave, poles, members):
    rows, channels = a.shape
    count = LANES // members
    return pl.pallas_call(
        functools.partial(summary_kernel, count, poles, members),
        grid=(channels // LANES,),
        in_specs=[
            pl.BlockSpec((rows, LANES), lambda j: (0, j)),
            pl.BlockSpec((rows, LANES), lambda j: (0, j)),
            pl.BlockSpec((count * poles, rows), lambda j: (j, 0)),
        ],
        out_specs=pl.BlockSpec((poles, LANES), lambda j: (0, j)),
        out_shape=jax.ShapeDtypeStruct((poles, channels), BF16),
        cost_estimate=pl.CostEstimate(
            flops=2 * rows * channels * poles * count,
            bytes_accessed=rows * channels * 8,
            transcendentals=0,
        ),
    )(a, b, leave)


def convolve(reverse, count, poles, members, blocks, line_of, emit, lag_ref, gain_ref, mask_ref,
             leave_ref, alive_ref, across_ref, alive_across_ref, enter_ref, base):
    for g in range(count):
        row = jnp.broadcast_to(lag_ref[g:g + 1, :], (BLOCK, LANES))
        matrix = pltpu.roll(row, 0, 1, stride=1, stride_axis=0)
        base[g * BLOCK:(g + 1) * BLOCK, :LANES] = matrix.astype(BF16)
    base[:, LANES:] = gain_ref[...]
    state = enter_ref[...]
    for step in range(blocks):
        b = blocks - 1 - step if reverse else step
        line = line_of(b)
        low = line.astype(BF16)
        mask = mask_ref[b]
        left = (base[...].reshape(count, BLOCK, LANES + poles) * mask[None]).reshape(
            count * BLOCK, LANES + poles
        )
        right = jnp.concatenate([low, state.astype(BF16)], axis=0)
        result = pick(
            jnp.dot(left, right, preferred_element_type=F32), count, BLOCK, members
        )
        emit(b, line, result)
        if step < blocks - 1:
            gone = leave_ref[...] * alive_ref[b:b + 1, :]
            fresh = pick(
                jnp.dot(gone.astype(BF16), low, preferred_element_type=F32), count, poles, members
            )
            state = across_ref[...] * alive_across_ref[b:b + 1, :] * state + fresh


def forward_kernel(count, poles, members, blocks, query, key, value, skip, lag, gain, mask, leave,
                   alive, across, alive_across, enter, filtered, gated, base):
    def rows(b):
        return pl.ds(b * BLOCK, BLOCK)

    def line_of(b):
        return (key[rows(b), :].astype(F32) * value[rows(b), :].astype(F32)).astype(BF16).astype(F32)

    def emit(b, line, result):
        result = result + skip[...] * line
        filtered[rows(b), :] = result
        gated[rows(b), :] = (query[rows(b), :].astype(F32) * result).astype(BF16)

    convolve(False, count, poles, members, blocks, line_of, emit, lag, gain, mask, leave, alive,
             across, alive_across, enter, base)


def backward_kernel(count, poles, members, blocks, query, key, value, grad_gated, filtered, skip,
                    lag, gain, mask, leave, alive, across, alive_across, enter, grad_query,
                    grad_key, grad_value, base):
    def rows(b):
        return pl.ds(b * BLOCK, BLOCK)

    def line_of(b):
        grad = grad_gated[rows(b), :]
        grad_query[rows(b), :] = (grad * filtered[rows(b), :]).astype(BF16)
        return grad * query[rows(b), :].astype(F32)

    def emit(b, line, result):
        result = result + skip[...] * line
        grad_key[rows(b), :] = (result * value[rows(b), :].astype(F32)).astype(BF16)
        grad_value[rows(b), :] = (result * key[rows(b), :].astype(F32)).astype(BF16)

    convolve(True, count, poles, members, blocks, line_of, emit, lag, gain, mask, leave, alive,
             across, alive_across, enter, base)


def run_conv(kernel, wide, skip, tables, enter, out_types, poles, members):
    rows, channels = wide[0].shape
    count = LANES // members
    blocks = rows // BLOCK
    column = pl.BlockSpec((rows, LANES), lambda j: (0, j))
    lag, gain, mask, leave, alive, across, alive_across = tables
    return pl.pallas_call(
        functools.partial(kernel, count, poles, members, blocks),
        grid=(channels // LANES,),
        in_specs=[column] * len(wide) + [
            pl.BlockSpec((1, LANES), lambda j: (0, j)),
            pl.BlockSpec((count, BLOCK), lambda j: (j, 0)),
            pl.BlockSpec((count * BLOCK, poles), lambda j: (j, 0)),
            pl.BlockSpec((blocks, BLOCK, BLOCK + poles), lambda j: (0, 0, 0)),
            pl.BlockSpec((count * poles, BLOCK), lambda j: (j, 0)),
            pl.BlockSpec((blocks, BLOCK), lambda j: (0, 0)),
            pl.BlockSpec((poles, LANES), lambda j: (0, j)),
            pl.BlockSpec((blocks, LANES), lambda j: (0, 0)),
            pl.BlockSpec((poles, LANES), lambda j: (0, j)),
        ],
        out_specs=[column] * len(out_types),
        out_shape=[jax.ShapeDtypeStruct((rows, channels), kind) for kind in out_types],
        scratch_shapes=[pltpu.VMEM((count * BLOCK, BLOCK + poles), BF16)],
        cost_estimate=pl.CostEstimate(
            flops=16 * rows * channels * BLOCK * 2, bytes_accessed=rows * channels * 14, transcendentals=0
        ),
    )(*wide, skip, lag, gain, mask, leave, alive, across, alive_across, enter)


def swap(value, flip, size):
    return lax.ppermute(value, "ctx", [(i, i ^ flip) for i in range(size)])


def gather_rows(own, size, me):
    if size != 8:
        return lax.all_gather(own, "ctx", axis=0, tiled=True)
    half = own.shape[0] // 2
    by_x, by_y = swap(own, 2, size), swap(own, 4, size)
    first, second = swap(by_x[:half], 4, size), swap(by_y[half:], 2, size)
    parts = {0: [own], 2: [by_x], 4: [by_y], 6: [first, second]}
    for flip in (0, 2, 4, 6):
        parts[flip ^ 1] = [swap(part, 1, size) for part in parts[flip]]
    rows, columns = own.shape
    whole = jnp.zeros((rows * size, columns), own.dtype)
    for flip, pieces in parts.items():
        at = (me ^ flip) * rows
        for piece in pieces:
            whole = lax.dynamic_update_slice(whole, piece, (at, 0))
            at = at + piece.shape[0]
    return whole


def after(value, *others):
    return lax.optimization_barrier((value, others))[0]


def gather_columns(own, axis):
    size, me = lax.axis_size(axis), lax.axis_index(axis)
    rows, width = own.shape
    from_left, from_right = [own], [own]
    for step in range(1, size):
        from_left.append(
            lax.ppermute(from_left[-1], axis, [(z, z + 1) for z in range(step - 1, size - 1)])
        )
        from_right.append(
            lax.ppermute(from_right[-1], axis, [(z + 1, z) for z in range(size - step)])
        )
    whole = jnp.zeros((rows, width * size), own.dtype)
    for ahead in range(size):
        piece = own
        if ahead:
            piece = jnp.where(me + ahead < size, from_right[ahead], from_left[size - ahead])
        whole = lax.dynamic_update_slice(whole, piece, (0, (me + ahead) % size * width))
    return whole, (from_left[1:2], from_right[1:2])


def scatter_columns(value, axis, before_last):
    size, me = lax.axis_size(axis), lax.axis_index(axis)
    width = value.shape[1] // size

    def own(position):
        start = jnp.clip(position, 0, size - 1) * width
        return lax.dynamic_slice_in_dim(value, start, width, axis=1).astype(F32)

    right = left = None
    for step in range(1, size):
        up, down = own(me + size - step), own(me - size + step)
        if step == size - 1:
            right, left = after((right, left), before_last)
        if right is not None:
            up, down = up + right.astype(F32), down + left.astype(F32)
        right = lax.ppermute(up.astype(BF16), axis, [(z, z + 1) for z in range(step)])
        left = lax.ppermute(
            down.astype(BF16), axis, [(size - 1 - z, size - 2 - z) for z in range(step)]
        )

    def finish(*others):
        last_right, last_left = after((right, left), others)
        return (own(me) + last_right.astype(F32) + last_left.astype(F32)).astype(BF16)

    return finish


def scatter_terms(grad_full, gated, size, me):
    contract = (((0,), (0,)), ((), ()))
    if size != 8:
        term = lax.dot_general(grad_full, gated, contract, preferred_element_type=F32).astype(BF16)
        return term, lambda term: lax.psum_scatter(term, "ctx", scatter_dimension=0, tiled=True).astype(F32)
    width = grad_full.shape[1] // size

    def chunk(flip):
        part = lax.dynamic_slice_in_dim(grad_full, (me ^ flip) * width, width, axis=1)
        return lax.dot_general(part, gated, contract, preferred_element_type=F32).astype(BF16)

    arriving = {flip: swap(chunk(flip ^ 1), 1, size) for flip in (6, 2, 4, 0)}
    terms = {flip: chunk(flip) for flip in (6, 2, 4, 0)}

    def finish(terms):
        half = gated.shape[1] // 2
        sums = {}
        for flip in (6, 2, 4, 0):
            sums[flip] = terms[flip].astype(F32) + arriving[flip].astype(F32)

        def route(columns, near, far):
            far_sum = sums[far][:, columns] + swap(sums[6][:, columns].astype(BF16), near, size).astype(F32)
            own_sum = sums[0][:, columns] + swap(sums[near][:, columns].astype(BF16), near, size).astype(F32)
            return own_sum + swap(far_sum.astype(BF16), far, size).astype(F32)

        return jnp.concatenate([route(slice(0, half), 2, 4), route(slice(half, None), 4, 2)], axis=1)

    return terms, finish


def local(
    query_in, key_in, value_in, residues, decay_time, skip_gain, out_proj, doc_lengths, grad_out
):
    rows, channels = query_in.shape
    filters, poles = residues.shape
    members = channels // filters
    blocks = rows // BLOCK
    size, me = lax.axis_size("ctx"), lax.axis_index("ctx")
    gathered = gather_rows(out_proj, size, me)
    grad_full, first_hop = gather_columns(grad_out, "grp")

    starts = jnp.cumsum(doc_lengths) - doc_lengths
    flat_ids = doc_index(starts, me * rows + jnp.arange(rows, dtype=jnp.int32))
    ids = flat_ids.reshape(blocks, BLOCK)
    firsts, lasts = ids[:, 0], ids[:, -1]
    before = doc_index(starts, me * rows - 1 + BLOCK * jnp.arange(blocks + 1, dtype=jnp.int32))
    following = doc_index(starts, me * rows + BLOCK * jnp.arange(1, blocks + 1, dtype=jnp.int32))
    ends = doc_index(starts, rows * jnp.arange(1, size + 1, dtype=jnp.int32) - 1)
    opens = doc_index(starts, rows * jnp.arange(size, dtype=jnp.int32))
    rate = 1.0 / decay_time
    beta = residues * jnp.sqrt(-jnp.expm1(-2.0 * rate))
    lags = jnp.arange(BLOCK, dtype=F32)
    rate_chan = jnp.repeat(rate.T, members, axis=1)
    response = jnp.sum(beta[:, :, None] * jnp.exp(-lags[None, None, :] * rate[:, :, None]), axis=1)
    mirrored = jnp.concatenate([response[:, :1], response[:, :0:-1]], axis=1)
    gain = beta[:, None, :] * jnp.exp(-(lags + 1.0)[None, :, None] * rate[:, None, :])
    gain_rev = beta[:, None, :] * jnp.exp(-(BLOCK - lags)[None, :, None] * rate[:, None, :])
    leave_rev = jnp.exp(-lags[None, :] * rate.reshape(-1, 1))
    leave = jnp.exp(-(BLOCK - 1.0 - lags)[None, :] * rate.reshape(-1, 1))
    across = jnp.exp(-BLOCK * rate_chan)
    same = ids[:, :, None] == ids[:, None, :]
    place = jnp.arange(BLOCK)
    causal = place[:, None] >= place[None, :]

    def mask_of(order, alive):
        tail = jnp.broadcast_to(alive[:, :, None], (blocks, BLOCK, poles))
        return jnp.concatenate([same & order[None], tail], axis=2).astype(BF16)

    def spread(flags):
        return jnp.broadcast_to(flags.astype(F32)[:, None], (blocks, LANES))

    forward = (
        mirrored,
        gain.reshape(-1, poles).astype(BF16),
        mask_of(causal, ids == before[:blocks, None]),
        leave,
        (ids == lasts[:, None]).astype(F32),
        across,
        spread(before[:blocks] == lasts),
    )
    backward = (
        response,
        gain_rev.reshape(-1, poles).astype(BF16),
        mask_of(causal.T, ids == following[:, None]),
        leave_rev,
        (ids == firsts[:, None]).astype(F32),
        across,
        spread(following == firsts),
    )
    steps = jnp.arange(rows, dtype=F32)
    whole_leave = jnp.exp(-(rows - 1.0 - steps)[None, :] * rate.reshape(-1, 1))
    whole_leave = (whole_leave * (flat_ids == flat_ids[-1])[None, :]).astype(BF16)
    whole_leave_rev = jnp.exp(-steps[None, :] * rate.reshape(-1, 1))
    whole_leave_rev = (whole_leave_rev * (flat_ids == flat_ids[0])[None, :]).astype(BF16)

    def incoming(state, distance, alive):
        everything = lax.all_gather(state, "ctx").astype(F32)
        gap = jnp.maximum(distance, 0).astype(F32) * rows
        weight = jnp.exp(-gap[:, None, None] * rate_chan[None])
        kept = (alive & (distance >= 0))[:, None, None]
        return jnp.sum(jnp.where(kept, weight * everything, 0.0), axis=0)

    devices = jnp.arange(size, dtype=jnp.int32)
    skip = skip_gain[None, :]
    state = summarize(key_in, value_in, whole_leave, poles, members)
    enter = incoming(state, me - 1 - devices, ends == before[0])
    enter = after(enter, first_hop)
    filtered, gated = run_conv(
        forward_kernel, (query_in, key_in, value_in), skip, forward, enter, (F32, BF16), poles, members
    )
    partial_value = lax.dot_general(
        gated, gathered, (((1,), (1,)), ((), ())), preferred_element_type=F32
    ).astype(BF16)
    terms, finish = scatter_terms(grad_full, gated, size, me)
    finish_mixed = scatter_columns(partial_value, "grp", terms)
    terms, grad_full, gathered = lax.optimization_barrier((terms, grad_full, gathered))
    grad_proj = finish(terms)
    grad_gated = jnp.dot(grad_full, gathered, preferred_element_type=F32)
    state = summarize(grad_gated, query_in, whole_leave_rev, poles, members)
    leaving = incoming(state, devices - 1 - me, opens == following[-1])
    grad_query, grad_key, grad_value = run_conv(
        backward_kernel, (query_in, key_in, value_in, grad_gated, filtered), skip, backward,
        leaving, (BF16, BF16, BF16), poles, members
    )
    mixed_out = finish_mixed(grad_query)
    return (mixed_out, grad_query, grad_key, grad_value, grad_proj)


def solution(mesh):
    return jax.shard_map(
        local,
        mesh=mesh,
        in_specs=(
            P("ctx", "grp"),
            P("ctx", "grp"),
            P("ctx", "grp"),
            P("grp", None),
            P("grp", None),
            P("grp"),
            P("ctx", "grp"),
            P(),
            P("ctx", "grp"),
        ),
        out_specs=(
            P("ctx", "grp"),
            P("ctx", "grp"),
            P("ctx", "grp"),
            P("ctx", "grp"),
            P("ctx", "grp"),
        ),
        check_vma=False,
    )
```
